512 devices in a mesh: blk: 256 (over z, y, x_lo, core), dp: 2 (over x_hi).
Axes of the slice: x: 4 (x_hi: 2, x_lo: 2; x = x_hi * 2 + x_lo), y: 4, z: 16, core: 2. Of those that a mesh axis runs over, the one named last changes fastest.
Arguments:
- acts: bfloat16 [2, 73728, 2048], P(None, ('blk', 'dp')), may hold values from -6 to 6
- cotangent: bfloat16 [2, 73728, 2048], P(None, ('blk', 'dp')), may hold values from -6 to 6
- w_gate: bfloat16 [256, 2048, 128], P('blk', 'dp'), may hold values from -0.125 to 0.125
- w_up: bfloat16 [256, 2048, 128], P('blk', 'dp'), may hold values from -0.125 to 0.125
- w_down: bfloat16 [256, 128, 2048], P('blk', None, 'dp'), may hold values from -0.078125 to 0.078125
- slab_layer: int32 [256], replicated, may hold values from 0 to 1
Outputs:
- grad_gate: bfloat16 [256, 2048, 128], P('blk', 'dp')
- grad_up: bfloat16 [256, 2048, 128], P('blk', 'dp')
- grad_down: bfloat16 [256, 128, 2048], P('blk', None, 'dp')
- acts_grad: bfloat16 [2, 73728, 2048], P(None, ('blk', 'dp'))
The draws below stay inside these ranges and needn't reach their ends.
All inputs are finite; a program needn't handle non-finite values.
Results may differ from the reference program's by a relative error of at most 0.0049.
Values may be sent and summed in bfloat16 or wider, within the bound.
No kernel may reach another device: no remote copies, remote signals or barrier semaphores. Data moves between devices by JAX's collectives and lax.ppermute only.
A program may use at most 64 MiB of HBM per device.

```python
import jax
import jax.numpy as jnp
from jax import lax

D = 2048
FF = 6144
SLAB = 128
LAYERS = 2
TICKS = 3
TOK_DEV = 144
ROWS = 73728
N_BLK = 256
N_DP = 2


def with_ends(array, own_key, least, largest):
    dims = array.shape
    place = [jax.random.randint(jax.random.fold_in(own_key, axis), (), 0, dims[axis]) for axis in range(len(dims))]
    array = array.at[tuple(place)].set(least)
    longest = dims.index(max(dims))
    place[longest] = (place[longest] + 1) % dims[longest]
    return array.at[tuple(place)].set(largest)


def block_levels(own_key, shape, cuts, low, largest):
    factor_of = 1.0
    for dim, parts in cuts:
        heights = jax.random.uniform(jax.random.fold_in(jax.random.fold_in(own_key, 6), dim), (parts,), jnp.float32, low / len(cuts), largest / len(cuts))
        factor_of = factor_of * jnp.repeat(jnp.exp(heights), shape[dim] // parts).reshape((-1,) + (1,) * (len(shape) - 1 - dim))
    return factor_of


def scatter_about(key, shape, deviation, limit, shards=(), held_as=jnp.bfloat16):
    drawn = jax.random.normal(key, shape, jnp.float32) * deviation
    if len(shards) > 0:
        drawn = block_levels(key, shape, shards, -0.22, 0.18) * drawn
    return jnp.clip(drawn, min=-limit, max=limit).astype(held_as)


def setup_inputs(seed: int = 0) -> dict:
    streams_of = jax.random.split(jax.random.key(seed), 7)
    acts = scatter_about(streams_of[0], (LAYERS, ROWS, D), 1.0, 6.0, ((1, 512),))
    cotangent = scatter_about(streams_of[1], (LAYERS, ROWS, D), 1.0, 6.0, ((1, 512),))
    w_gate = scatter_about(streams_of[2], (N_BLK, D, SLAB), D ** -0.5, 0.125, ((0, 256), (1, 2)))
    w_up = scatter_about(streams_of[3], (N_BLK, D, SLAB), D ** -0.5, 0.125, ((0, 256), (1, 2)))
    w_down = scatter_about(streams_of[4], (N_BLK, SLAB, D), FF ** -0.5, 0.078125, ((0, 256), (2, 2)))
    slab_layer = with_ends(jax.random.randint(streams_of[5], (N_BLK,), 0, LAYERS), jax.random.fold_in(streams_of[5], 1), 0, LAYERS - 1).astype(jnp.int32)
    return dict(acts=acts, cotangent=cotangent, w_gate=w_gate, w_up=w_up, w_down=w_down, slab_layer=slab_layer)


def slab_terms(rows_x, rows_g, w_gate, w_up, w_down):
    gate = jnp.dot(rows_x, w_gate, preferred_element_type=jnp.float32)
    upward = jnp.dot(rows_x, w_up, preferred_element_type=jnp.float32)
    sigmoid_gate = jax.nn.sigmoid(gate)
    activated = gate * sigmoid_gate
    hidden = (activated * upward).astype(jnp.bfloat16)
    by_units = (((1,), (1,)), ((), ()))
    by_rows = (((0,), (0,)), ((), ()))
    hidden_grad = lax.dot_general(rows_g, w_down, by_units, preferred_element_type=jnp.float32)
    up_in = (hidden_grad * activated).astype(jnp.bfloat16)
    gate_in = (hidden_grad * upward * sigmoid_gate * (1.0 + gate * (1.0 - sigmoid_gate))).astype(jnp.bfloat16)
    grad_gate = lax.dot_general(rows_x, gate_in, by_rows, preferred_element_type=jnp.float32)
    grad_upw = lax.dot_general(rows_x, up_in, by_rows, preferred_element_type=jnp.float32)
    grad_down = lax.dot_general(hidden, rows_g, by_rows, preferred_element_type=jnp.float32)
    input_grad = lax.dot_general(gate_in, w_gate, by_units, preferred_element_type=jnp.float32)
    input_grad = input_grad + lax.dot_general(up_in, w_up, by_units, preferred_element_type=jnp.float32)
    return (grad_gate, grad_upw, grad_down), input_grad


def reference(acts, cotangent, w_gate, w_up, w_down, slab_layer):
    group = TOK_DEV * N_DP
    zero_index = jnp.zeros((), jnp.int32)

    def visit(total, slab):
        layer = slab_layer[slab].astype(jnp.int32)
        gate_w = lax.dynamic_index_in_dim(w_gate, slab, 0, keepdims=False)
        up_w = lax.dynamic_index_in_dim(w_up, slab, 0, keepdims=False)
        down_w = lax.dynamic_index_in_dim(w_down, slab, 0, keepdims=False)
        sums = None
        for tick in range(TICKS):
            start = (((slab + tick) % N_BLK) * group).astype(jnp.int32)
            rows_x = lax.dynamic_slice(acts, (layer, start, zero_index), (1, group, D))[0]
            rows_g = lax.dynamic_slice(cotangent, (layer, start, zero_index), (1, group, D))[0]
            terms, input_grad = slab_terms(rows_x, rows_g, gate_w, up_w, down_w)
            sums = terms if sums is None else (sums[0] + terms[0], sums[1] + terms[1], sums[2] + terms[2])
            current = lax.dynamic_slice(total, (layer, start, zero_index), (1, group, D))
            total = lax.dynamic_update_slice(total, current + input_grad[None], (layer, start, zero_index))
        return total, sums

    start_total = jnp.zeros((LAYERS, ROWS, D), jnp.float32)
    total, sums = lax.scan(visit, start_total, jnp.arange(N_BLK, dtype=jnp.int32))
    return (sums[0].astype(jnp.bfloat16), sums[1].astype(jnp.bfloat16), sums[2].astype(jnp.bfloat16), total.astype(jnp.bfloat16))
```

```python
import functools

import jax
import jax.numpy as jnp
from jax import lax
from jax.experimental import pallas as pl
from jax.experimental.pallas import tpu as pltpu
from jax.sharding import PartitionSpec as P

F32, BF16 = jnp.float32, jnp.bfloat16
BY_LAST = (((1,), (1,)), ((), ()))
BY_FIRST = (((0,), (0,)), ((), ()))
VMEM = pl.BlockSpec(memory_space=pltpu.VMEM)
SMEM = pl.BlockSpec(memory_space=pltpu.SMEM)


def step_x(b, d, by):
    x = (2 * d + (b // 2) % 2 + by) % 4
    return x % 2, x // 2


def hop(by, chips):
    def target(b, d):
        lo, hi = step_x(b, d, by)
        return (b + 2 * chips, hi)

    return target


def along_row(by):
    def target(b, d):
        lo, hi = step_x(b, d, by(b))
        return ((b // 4) * 4 + 2 * lo + b % 2, hi)

    return target


def sent(array, even, odd, mesh_sizes):
    blk, dp = mesh_sizes
    pairs = []
    for b in range(blk):
        for d in range(dp):
            rule = odd if b % 2 else even
            if rule is not None:
                tb, td = rule(b, d)
                pairs.append((b * dp + d, (tb % blk) * dp + td))
    return lax.ppermute(array, ("blk", "dp"), pairs)


def whereabouts():
    b = lax.axis_index("blk")
    return b, lax.axis_index("dp"), b % 2, (b // 2) % 2


def pack_kernel(gate_ref, up_ref, down_ref, out_ref):
    out_ref[:, :128] = gate_ref[0]
    out_ref[:, 128:256] = up_ref[0]
    out_ref[:, 256:] = down_ref[0].T


def slab_terms(x_ref, g_ref, s_ref):
    both = jnp.dot(x_ref[...], s_ref[:, :256], preferred_element_type=F32)
    hidden_grad = jnp.dot(g_ref[...], s_ref[:, 256:], preferred_element_type=F32)
    gate, up = both[:, :128], both[:, 128:]
    sig = jax.nn.sigmoid(gate)
    act = gate * sig
    hidden = (act * up).astype(BF16)
    up_in = (hidden_grad * act).astype(BF16)
    gate_in = (hidden_grad * up * sig * (1.0 + gate * (1.0 - sig))).astype(BF16)
    both_in = jnp.concatenate([gate_in, up_in], axis=1)
    return both_in, hidden


def first_kernel(
    layer_ref, x_ref, g_ref, swap_ref, own_ref, near_ref, far_ref,
    sums_ref, out_ref, dx_own_ref, dx_swap_ref,
    slab, xs, gs,
):
    b, d, core, lo = whereabouts()
    n = lax.axis_size("blk")
    rows = x_ref.shape[1]
    half = own_ref.shape[0]
    here = pl.multiple_of(d * half, half)
    there = pl.multiple_of((1 - d) * half, half)

    @pl.when(core == 0)
    def _():
        slab[pl.ds(here, half), :] = own_ref[...]
        slab[pl.ds(there, half), :] = near_ref[...]

    @pl.when(core == 1)
    def _():
        first = pl.multiple_of(((d + lo) % 2) * half, half)
        second = pl.multiple_of(((d + lo + 1) % 2) * half, half)
        slab[pl.ds(first, half), :] = near_ref[...]
        slab[pl.ds(second, half), :] = far_ref[...]

    layer = layer_ref[(b - 2 * core + n) % n]
    xs[:rows] = x_ref[layer]
    gs[:rows] = g_ref[layer]
    xs[rows:] = swap_ref[0]
    gs[rows:] = swap_ref[1]
    both_in, hidden = slab_terms(xs, gs, slab)
    dx = lax.dot_general(both_in, slab[:, :256], BY_LAST, preferred_element_type=F32)
    dx_own_ref[...] = dx[:rows]
    dx_swap_ref[...] = dx[rows:].astype(BF16)
    sums_ref[:256] = lax.dot_general(both_in, xs[...], BY_FIRST, preferred_element_type=F32)
    sums_ref[256:] = lax.dot_general(hidden, gs[...], BY_FIRST, preferred_element_type=F32)
    pick = pl.multiple_of(((d + lo) % 2) * half, half)
    out_ref[...] = sums_ref[:, pl.ds(pick, half)].astype(BF16)


def second_kernel(
    layer_ref, x_ref, g_ref, guest_ref, own_ref, near_ref, relayed_ref, sums_ref,
    mine_ref, out_ref, dx_guest_ref, dx_own_ref,
    slab, xs, gs, total,
):
    b, d, core, lo = whereabouts()
    half = own_ref.shape[0]
    here = pl.multiple_of(d * half, half)
    there = pl.multiple_of((1 - d) * half, half)
    slab[pl.ds(here, half), :] = own_ref[...]

    @pl.when(core == 0)
    def _():
        slab[pl.ds(there, half), :] = near_ref[...]
        xs[...] = guest_ref[0]
        gs[...] = guest_ref[1]

    @pl.when(core == 1)
    def _():
        slab[pl.ds(there, half), :] = relayed_ref[...]
        layer = layer_ref[b]
        xs[...] = x_ref[layer]
        gs[...] = g_ref[layer]

    both_in, hidden = slab_terms(xs, gs, slab)
    total[:256] = lax.dot_general(both_in, xs[...], BY_FIRST, preferred_element_type=F32)
    total[256:] = lax.dot_general(hidden, gs[...], BY_FIRST, preferred_element_type=F32)

    @pl.when(core == 0)
    def _():
        total[...] += sums_ref[...]

    mine_ref[...] = total[:, pl.ds(here, half)]
    out_ref[...] = total[:, pl.ds(there, half)].astype(BF16)
    dx = lax.dot_general(both_in, slab[:, :256], BY_LAST, preferred_element_type=F32)
    dx_guest_ref[...] = dx.astype(BF16)
    dx_own_ref[...] = jnp.where(core == 1, dx, 0.0)


def relay_kernel(sums_ref, got_ref, out_ref):
    b, d, core, lo = whereabouts()
    half = got_ref.shape[1]

    @pl.when(core == 0)
    def _():
        out_ref[...] = got_ref[...]

    @pl.when(core == 1)
    def _():
        pick = pl.multiple_of(((d + lo + 1) % 2) * half, half)
        out_ref[...] = (sums_ref[:, pl.ds(pick, half)] + got_ref[...].astype(F32)).astype(BF16)


def final_kernel(mine_ref, a_ref, b_ref, gate_ref, up_ref, down_ref):
    total = mine_ref[...] + a_ref[...].astype(F32) + b_ref[...].astype(F32)
    gate_ref[0] = total[:128].T.astype(BF16)
    up_ref[0] = total[128:256].T.astype(BF16)
    down_ref[0] = total[256:].astype(BF16)


def tokens_kernel(layer_ref, dx_own_ref, swap_ref, guest_ref, dx_late_ref, out_ref):
    b, d, core, lo = whereabouts()
    n = lax.axis_size("blk")
    own = layer_ref[(b - 2 * core + n) % n]
    mid = layer_ref[(b - 1 + n) % n]
    late = layer_ref[(b - 2 * (1 - core) + n) % n]
    for l in range(out_ref.shape[0]):
        out_ref[l] = (
            jnp.where(own == l, dx_own_ref[...], 0.0)
            + jnp.where(mid == l, swap_ref[...].astype(F32), 0.0)
            + jnp.where(late == l, guest_ref[...].astype(F32) + dx_late_ref[...], 0.0)
        ).astype(BF16)


def tile(shape, dtype):
    return jax.ShapeDtypeStruct(shape, dtype)


def call(body, outs, operands, scratch=(), flops=0):
    moved = sum(a.size * a.dtype.itemsize for a in operands)
    specs = [SMEM if a.dtype == jnp.int32 else VMEM for a in operands]
    return pl.pallas_call(
        body,
        out_shape=outs,
        in_specs=specs,
        out_specs=jax.tree.map(lambda _: VMEM, outs),
        scratch_shapes=list(scratch),
        cost_estimate=pl.CostEstimate(flops=flops, bytes_accessed=moved, transcendentals=0),
    )(*operands)


def on_device(acts, cotangent, w_gate, w_up, w_down, slab_layer, sizes):
    layers, rows, width = acts.shape
    half = w_gate.shape[1]
    units = w_gate.shape[2]
    send = functools.partial(sent, mesh_sizes=sizes)
    b = lax.axis_index("blk")
    n = sizes[0]

    def swap_core(b, d):
        return (b ^ 1, d)

    def swap_dp(b, d):
        return (b, 1 - d)

    own = call(pack_kernel, tile((half, 3 * units), BF16), (w_gate, w_up, w_down))
    near = send(own, swap_dp, hop(-1, 1))
    far = send(own, None, hop(1, 1))

    def rows_of(layer):
        pick = lambda a: lax.dynamic_index_in_dim(a, layer, 0, keepdims=False)
        return jnp.stack([pick(acts), pick(cotangent)])

    swap = send(rows_of(slab_layer[(b - 1) % n]), swap_core, swap_core)
    guest = send(rows_of(slab_layer[(b - 2) % n]), hop(-1, -1), None)
    relayed = send(near, None, hop(-1, -1))

    flops = 16 * rows * width * units
    sums, near_sum, dx_own, dx_swap = call(
        first_kernel,
        (
            tile((3 * units, width), F32), tile((3 * units, half), BF16),
            tile((rows, width), F32), tile((rows, width), BF16),
        ),
        (slab_layer, acts, cotangent, swap, own, near, far),
        (
            pltpu.VMEM((width, 3 * units), BF16),
            pltpu.VMEM((2 * rows, width), BF16), pltpu.VMEM((2 * rows, width), BF16),
        ),
        2 * flops,
    )
    got_near = send(near_sum, None, hop(1, -1))
    dx_swapped = send(dx_swap, swap_core, swap_core)
    mine, own_sum, dx_guest, dx_late = call(
        second_kernel,
        (
            tile((3 * units, half), F32), tile((3 * units, half), BF16),
            tile((rows, width), BF16), tile((rows, width), F32),
        ),
        (slab_layer, acts, cotangent, guest, own, near, relayed, sums),
        (
            pltpu.VMEM((width, 3 * units), BF16),
            pltpu.VMEM((rows, width), BF16), pltpu.VMEM((rows, width), BF16),
            pltpu.VMEM((3 * units, width), F32),
        ),
        flops,
    )
    passed = send(own_sum, along_row(lambda b: -1 if (b // 2) % 2 else 1), hop(-1, 1))
    dx_back = send(dx_guest, hop(1, 1), None)
    onward = call(relay_kernel, tile((3 * units, half), BF16), (sums, passed))
    got_far = send(onward, along_row(lambda b: 1 if (b // 2) % 2 else -1), hop(-1, -1))
    acts_grad = call(
        tokens_kernel, tile(acts.shape, BF16), (slab_layer, dx_own, dx_swapped, dx_back, dx_late)
    )
    grads = call(
        final_kernel,
        (tile((1, half, units), BF16), tile((1, half, units), BF16), tile((1, units, half), BF16)),
        (mine, got_near, got_far),
    )
    return (*grads, acts_grad)


def solution(mesh):
    in_specs = (
        P(None, ("blk", "dp"), None),
        P(None, ("blk", "dp"), None),
        P("blk", "dp", None),
        P("blk", "dp", None),
        P("blk", None, "dp"),
        P(),
    )
    out_specs = (
        P("blk", "dp", None),
        P("blk", "dp", None),
        P("blk", None, "dp"),
        P(None, ("blk", "dp"), None),
    )
    body = functools.partial(on_device, sizes=(mesh.shape["blk"], mesh.shape["dp"]))
    return jax.shard_map(
        body, mesh=mesh, in_specs=in_specs, out_specs=out_specs, check_vma=False
    )
```
